256 devices in a mesh: slab: 4 (over y), pencil: 64 (over z, x, core).
Axes of the slice: x: 4, y: 4, z: 8, core: 2. Of those that a mesh axis runs over, the one named last changes fastest.
Arguments:
- spectrum: float32 [2, 8, 2048, 4096], P(None, 'slab', 'pencil'), may hold values from -6 to 6
Outputs:
- rendered: float32 [4, 8, 4096], P(None, 'slab', 'pencil')
The draws below stay inside these ranges and needn't reach their ends.
All inputs are finite; a program needn't handle non-finite values.
Results may differ from the reference program's by a relative error of at most 0.0003.
Values sent between devices are 32-bit elements; how exact they have to be, the bound alone decides.
No kernel may reach another device: no remote copies, remote signals or barrier semaphores. Data moves between devices by JAX's collectives and lax.ppermute only.
A program may use at most 64 MiB of HBM per device.

```python
import math
import jax
import jax.numpy as jnp
from jax import lax

N = 4096
NY = 8
KZ = 2048


def block_scale(own_key, extent, cuts, least, largest):
    level, own = 1.0, jax.random.fold_in(own_key, 6)
    for dim, shards_of in cuts:
        heights = jnp.exp(jax.random.uniform(jax.random.fold_in(own, dim), (shards_of,), jnp.float32, least / len(cuts), largest / len(cuts)))
        level = level * jnp.repeat(heights, extent[dim] // shards_of).reshape([-1 if axis == dim else 1 for axis in range(len(extent))])
    return level


def noise(own_key, extent, scale, reach, cuts=(), kind=jnp.bfloat16):
    array = scale * jax.random.normal(own_key, extent, jnp.float32)
    if cuts:
        array = array * block_scale(own_key, extent, cuts, -0.22, 0.18)
    return jnp.clip(array, -reach, reach).astype(kind)


def setup_inputs(seed: int = 0) -> dict:
    keys = jax.random.split(jax.random.key(seed), 2)
    spectrum = noise(keys[0], (2, NY, KZ, N), 0.7071, 6.0, ((1, 4), (2, 64)), jnp.float32)
    return {"spectrum": spectrum}


def field_plane(spectrum, plane_index):
    planes = lax.dynamic_index_in_dim(spectrum, plane_index, axis=1, keepdims=False)
    coeffs = lax.complex(planes[0], planes[1])
    line_field = jnp.fft.ifft(coeffs, axis=1) * math.sqrt(N)
    weights = jnp.where(jnp.arange(KZ) == 0, 1.0, 2.0).astype(planes.dtype)
    scaled = line_field * weights[:, None] / math.sqrt(N)
    padded = jnp.concatenate([scaled, jnp.zeros_like(scaled)], axis=0)
    values = jnp.real(jnp.fft.ifft(padded, axis=0)) * N
    return values.T

def render_plane(previous, current, following):
    shading = 1.0 + 0.5 * jnp.tanh(0.5 * (following - previous))
    extinction = current * current / N
    opacity_cell = 1.0 - jnp.exp(-extinction)
    before = jnp.cumsum(extinction, axis=0) - extinction
    weight = jnp.exp(-before) * opacity_cell * shading
    red_part = jax.nn.sigmoid(3.0 * current)
    green_part = 0.5 * jnp.exp(-current * current)
    blue_part = 1.0 - red_part
    channels = [lax.optimization_barrier(jnp.sum(weight * red_part, axis=0)), lax.optimization_barrier(jnp.sum(weight * green_part, axis=0)), lax.optimization_barrier(jnp.sum(weight * blue_part, axis=0)), 1.0 - jnp.exp(-lax.optimization_barrier(jnp.sum(extinction, axis=0)))]
    return jnp.stack(channels)

def reference(spectrum):
    last_plane = field_plane(spectrum, NY - 1)
    first_plane = field_plane(spectrum, 0)

    def advance(carry, plane_index):
        previous, current = carry
        following = field_plane(spectrum, (plane_index + 1) % NY)
        return ((current, following), render_plane(previous, current, following))
    finished, image_rows = lax.scan(advance, (last_plane, first_plane), jnp.arange(NY, dtype=jnp.int32))
    return jnp.transpose(image_rows, (1, 0, 2))
```

```python
import math

import numpy as np

import jax
import jax.numpy as jnp
from jax import lax
from jax.experimental import pallas as pl
from jax.experimental.pallas import tpu as pltpu
from jax.sharding import PartitionSpec as P

N = 4096
AXES = ("slab", "pencil")
F32 = jnp.float32
BF16 = jnp.bfloat16


def split_np(table):
    high = table.astype(np.float32).astype(BF16)
    low = (table - high.astype(np.float64)).astype(np.float32).astype(BF16)
    return high, low


def split(value):
    high = value.astype(BF16)
    low = (value - high.astype(F32)).astype(BF16)
    return high, low


def complex_block(phase):
    cosine, sine = np.cos(phase), np.sin(phase)
    return np.block([[cosine, -sine], [sine, cosine]])


def x_tables():
    blocks = np.arange(256)
    matrix = complex_block(2 * np.pi * (blocks[:, None] * blocks[None, :] % 256) / 256)
    fine = 2 * np.pi * (np.arange(16)[:, None] * blocks[None, :] % N) / N
    twist = np.stack([np.cos(fine), np.sin(fine)], axis=1).reshape(32, 256) / 64
    return (twist.astype(np.float32),) + split_np(matrix)


def z_tables():
    outer = np.arange(128)[:, None] * np.arange(64)[None, :]
    first = complex_block(2 * np.pi * (outer % 128) / 128) / 32
    fine = 2 * np.pi * (np.arange(128)[:, None] * (np.arange(128) % 32)[None, :] % N) / N
    twist = np.stack([np.cos(fine), np.sin(fine)])
    short = 2 * np.pi * (np.arange(32)[:, None] * np.arange(32)[None, :] % 32) / 32
    second = np.concatenate(
        [np.kron(np.eye(4), np.cos(short)), -np.kron(np.eye(4), np.sin(short))], axis=1
    )
    first_high, first_low = split_np(first)
    first_both = np.concatenate([first_high, first_high], axis=1)
    return (first_both, first_low, twist.astype(np.float32)) + split_np(second)


def four(a, b, c, d):
    (ar, ai), (br, bi), (cr, ci), (dr, di) = a, b, c, d
    er, ei, fr, fi = ar + cr, ai + ci, ar - cr, ai - ci
    gr, gi, hr, hi = br + dr, bi + di, br - dr, bi - di
    return [(er + gr, ei + gi), (fr - hi, fi + hr), (er - gr, ei - gi), (fr + hi, fi - hr)]


def turned(value, steps):
    re, im = value
    if steps == 0:
        return value
    if steps == 4:
        return (-im, re)
    half = math.sqrt(0.5)
    if steps == 2:
        return ((re - im) * half, (re + im) * half)
    if steps == 6:
        return ((-re - im) * half, (re - im) * half)
    c, s = math.cos(math.pi * steps / 8), math.sin(math.pi * steps / 8)
    return (re * c - im * s, re * s + im * c)


def x_kernel(data, twist, high_w, low_w, out, high_t, low_t):
    for y in range(2):
        for half in range(2):
            for tile in range(2):
                rows = pl.ds(16 * half, 16)
                cells = [
                    tuple(
                        data[part, y, rows, pl.ds(256 * t + 128 * tile, 128)] for part in range(2)
                    )
                    for t in range(16)
                ]
                middle = [four(*(cells[4 * t1 + t0] for t1 in range(4))) for t0 in range(4)]
                for k1 in range(4):
                    ends = four(*(turned(middle[t0][k1], t0 * k1) for t0 in range(4)))
                    for k0 in range(4):
                        fine = k1 + 4 * k0
                        re, im = ends[k0]
                        lanes = pl.ds(128 * tile, 128)
                        c = twist[pl.ds(2 * fine, 1), lanes]
                        s = twist[pl.ds(2 * fine + 1, 1), lanes]
                        for part, value in enumerate((re * c - im * s, re * s + im * c)):
                            high, low = split(value)
                            at = pl.ds(64 * (fine // 8) + 32 * y + 16 * half, 16)
                            columns = pl.ds(256 * part + 128 * tile, 128)
                            high_t[fine % 8, at, columns] = high
                            low_t[fine % 8, at, columns] = low

    def send(fine, carry):
        high, low = high_t[fine], low_t[fine]
        for part in range(2):
            w_rows = pl.ds(256 * part, 256)
            value = across(high_w[w_rows], high) + across(high_w[w_rows], low)
            value = value + across(low_w[w_rows], high)
            out[pl.ds(8 * part + fine, 256, stride=16), :] = value
        return carry

    lax.fori_loop(0, 8, send, 0)


def across(left, right):
    return lax.dot_general(left, right, (((1,), (1,)), ((), ())), preferred_element_type=F32)


def straight(left, right):
    return lax.dot_general(left, right, (((1,), (0,)), ((), ())), preferred_element_type=F32)


def z_kernel(got, first_both, first_low, twist, second_high, second_low, out, field):
    lane = lax.broadcasted_iota(jnp.int32, (64, 128), 1)
    mode = lax.broadcasted_iota(jnp.int32, (64, 128), 0)
    weight = jnp.where((mode == 0) & (lane % 32 == 0), 0.5, 1.0).astype(F32)

    def transform(slab, carry):
        for pair in range(4):
            parts = []
            for part in range(2):
                parts.append(
                    jnp.concatenate(
                        [
                            got[pl.ds(slab * 1024 + 8 * part + 2 * pair + k, 64, stride=16), :]
                            * weight
                            for k in range(2)
                        ],
                        axis=1,
                    )
                )
            high, low = split(jnp.concatenate(parts, axis=0))
            lines = straight(first_both[...], jnp.concatenate([high, low], axis=0))
            lines = lines + straight(first_low[...], high)
            c, s = twist[0], twist[1]
            turned_parts = []
            for k in range(2):
                re = lines[:128, 128 * k : 128 * k + 128]
                im = lines[128:, 128 * k : 128 * k + 128]
                turned_parts.append(jnp.concatenate([re * c - im * s, re * s + im * c], axis=1))
            high, low = split(jnp.concatenate(turned_parts, axis=0))
            value = across(second_high[...], high) + across(second_high[...], low)
            value = value + across(second_low[...], high)
            for k in range(2):
                for far in range(2):
                    for y in range(2):
                        row = 64 * far + 32 * y
                        field[8 * far + 2 * pair + k, 2 * slab + y] = value[
                            row : row + 32, 128 * k : 128 * k + 128
                        ]
        return carry

    lax.fori_loop(0, 4, transform, 0)
    first_half = lax.broadcasted_iota(jnp.int32, (32, 128), 1) < 64

    def render(slab, carry):
        planes = []
        for odd in range(2):
            y = 2 * slab + odd
            before, after = (y + 7) % 8, (y + 1) % 8
            zero = jnp.zeros((32, 128), F32)
            clear, depth, total, tilted, glow = jnp.ones((32, 128), F32), zero, zero, zero, zero
            for x in range(16):
                value = field[x, y]
                shading = 1.0 + 0.5 * jnp.tanh(0.5 * (field[x, after] - field[x, before]))
                square = value * value
                extinction = square * (1.0 / N)
                passed = jnp.exp(-extinction)
                weight = clear * (1.0 - passed) * shading
                clear = clear * passed
                depth = depth + extinction
                total = total + weight
                tilted = tilted + weight * jnp.tanh(1.5 * value)
                glow = glow + weight * jnp.exp(-square)
            red = 0.5 * (total + tilted)
            planes.append((red, 0.5 * glow, total - red, depth))
        for channel in range(4):
            low, high = planes[0][channel], planes[1][channel]
            mixed = (
                jnp.where(first_half, low, pltpu.roll(high, 64, 1)),
                jnp.where(first_half, pltpu.roll(low, 64, 1), high),
            )
            for core in range(2):
                out[pl.ds(slab * 256 + 4 * core + channel, 32, stride=8), :] = mixed[core]
        return carry

    lax.fori_loop(0, 4, render, 0)


def blend_kernel(got, out):
    depth = got[pl.ds(3, 256, stride=4), :]
    row = lax.broadcasted_iota(jnp.int32, (256, 256), 0)
    col = lax.broadcasted_iota(jnp.int32, (256, 256), 1)
    earlier = (col < row).astype(BF16)
    high = depth.astype(BF16)
    rest = depth - high.astype(F32)
    middle = rest.astype(BF16)
    low = (rest - middle.astype(F32)).astype(BF16)
    before = straight(earlier, high) + straight(earlier, middle) + straight(earlier, low)
    clear = jnp.exp(-before)
    rows = [
        jnp.sum(clear * got[pl.ds(channel, 256, stride=4), :], axis=0, keepdims=True)
        for channel in range(3)
    ]
    rows.append(1.0 - jnp.exp(-jnp.sum(depth, axis=0, keepdims=True)))
    for channel in range(4):
        for y in range(2):
            out[channel, pl.ds(y, 1), :] = rows[channel][:, 64 * y : 64 * y + 64]


def vmem_call(kernel, out_shape, scratch=()):
    return pl.pallas_call(
        kernel, out_shape=jax.ShapeDtypeStruct(out_shape, F32), scratch_shapes=scratch
    )


def local(spectrum):
    tables = [jnp.asarray(table) for table in x_tables()]
    sent = vmem_call(
        x_kernel,
        (4096, 128),
        [pltpu.VMEM((8, 128, 512), BF16), pltpu.VMEM((8, 128, 512), BF16)],
    )(spectrum, *tables)
    got = lax.all_to_all(sent.reshape(256, 16, 128), AXES, split_axis=0, concat_axis=0, tiled=True)
    tables = [jnp.asarray(table) for table in z_tables()]
    sent = vmem_call(z_kernel, (1024, 128), [pltpu.VMEM((16, 8, 32, 128), F32)])(
        got.reshape(4096, 128), *tables
    )
    got = lax.all_to_all(sent.reshape(256, 4, 128), AXES, split_axis=0, concat_axis=0, tiled=True)
    return vmem_call(blend_kernel, (4, 2, 64))(got.reshape(1024, 128))


def solution(mesh):
    return jax.shard_map(
        local,
        mesh=mesh,
        in_specs=(P(None, "slab", "pencil", None),),
        out_specs=P(None, "slab", "pencil"),
        check_vma=False,
    )
```

```python
import math

import numpy as np

import jax
import jax.numpy as jnp
from jax import lax
from jax.experimental import pallas as pl
from jax.experimental.pallas import tpu as pltpu
from jax.sharding import PartitionSpec as P

N = 4096
LOG2E = math.log2(math.e)
AXES = ("slab", "pencil")
F32 = jnp.float32
BF16 = jnp.bfloat16


def split_np(table):
    high = table.astype(np.float32).astype(BF16)
    low = (table - high.astype(np.float64)).astype(np.float32).astype(BF16)
    return high, low


def split(value):
    high = value.astype(BF16)
    low = (value - high.astype(F32)).astype(BF16)
    return high, low


def complex_block(phase):
    cosine, sine = np.cos(phase), np.sin(phase)
    return np.block([[cosine, -sine], [sine, cosine]])


def x_tables():
    blocks = np.arange(256)
    matrix = complex_block(2 * np.pi * (blocks[:, None] * blocks[None, :] % 256) / 256)
    fine = 2 * np.pi * (np.arange(16)[:, None] * blocks[None, :] % N) / N
    twist = np.stack([np.cos(fine), np.sin(fine)], axis=1).reshape(32, 256)
    return (twist.astype(np.float32),) + split_np(matrix)


def z_tables():
    outer = np.arange(128)[:, None] * np.arange(64)[None, :]
    first = complex_block(2 * np.pi * (outer % 128) / 128) / 4096
    fine = 2 * np.pi * (np.arange(128)[:, None] * (np.arange(128) % 32)[None, :] % N) / N
    twist = np.stack([np.cos(fine), np.sin(fine)])
    short = 2 * np.pi * (np.arange(32)[:, None] * np.arange(32)[None, :] % 32) / 32
    second = np.concatenate(
        [np.kron(np.eye(4), np.cos(short)), -np.kron(np.eye(4), np.sin(short))], axis=1
    )
    first_high, first_low = split_np(first)
    first_both = np.concatenate([first_high, first_high], axis=1)
    second_all = np.concatenate(split_np(second), axis=0)
    return (first_both, first_low, twist.astype(np.float32), second_all)


def four(a, b, c, d):
    (ar, ai), (br, bi), (cr, ci), (dr, di) = a, b, c, d
    er, ei, fr, fi = ar + cr, ai + ci, ar - cr, ai - ci
    gr, gi, hr, hi = br + dr, bi + di, br - dr, bi - di
    return [(er + gr, ei + gi), (fr - hi, fi + hr), (er - gr, ei - gi), (fr + hi, fi - hr)]


def turned(value, steps):
    re, im = value
    if steps == 0:
        return value
    if steps == 4:
        return (-im, re)
    half = math.sqrt(0.5)
    if steps == 2:
        return ((re - im) * half, (re + im) * half)
    if steps == 6:
        return ((-re - im) * half, (re - im) * half)
    c, s = math.cos(math.pi * steps / 8), math.sin(math.pi * steps / 8)
    return (re * c - im * s, re * s + im * c)


def x_kernel(
    data, twist_hbm, high_hbm, low_hbm, out, cells_v, twist, high_w, low_w, high_t, low_t, sems
):
    copies = [pltpu.make_async_copy(twist_hbm, twist, sems.at[0])]
    for y in range(2):
        for half in range(2):
            rows = pl.ds(16 * half, 16)
            copies.append(
                pltpu.make_async_copy(
                    data.at[:, y, rows, :], cells_v.at[:, y, rows, :], sems.at[1 + 2 * y + half]
                )
            )
    copies.append(pltpu.make_async_copy(high_hbm, high_w, sems.at[5]))
    copies.append(pltpu.make_async_copy(low_hbm, low_w, sems.at[6]))
    for copy in copies:
        copy.start()

    def stage(y, half, tile):
        rows, lanes = pl.ds(16 * half, 16), pl.ds(128 * tile, 128)
        cells = [
            tuple(cells_v[part, y, rows, pl.ds(256 * t + 128 * tile, 128)] for part in range(2))
            for t in range(16)
        ]
        middle = [four(*(cells[4 * t1 + t0] for t1 in range(4))) for t0 in range(4)]
        for k1 in range(4):
            ends = four(*(turned(middle[t0][k1], t0 * k1) for t0 in range(4)))
            for k0 in range(4):
                fine = k1 + 4 * k0
                value = ends[k0]
                if fine:
                    re, im = value
                    c = twist[pl.ds(2 * fine, 1), lanes]
                    s = twist[pl.ds(2 * fine + 1, 1), lanes]
                    value = (re * c - im * s, re * s + im * c)
                for part in range(2):
                    high, low = split(value[part])
                    at = pl.ds(32 * fine + 16 * half, 16)
                    columns = pl.ds(256 * part + 128 * tile, 128)
                    high_t[y, at, columns] = high
                    low_t[y, at, columns] = low

    def send(y, pair, part):
        rows, w_rows = pl.ds(256 * pair, 256), pl.ds(256 * part, 256)
        high, low = high_t[y, rows], low_t[y, rows]
        value = across(high_w[w_rows], high) + across(low_w[w_rows], high)
        value = value + across(high_w[w_rows], low)
        for k in range(2):
            row = 8 * part + 4 * y + 2 * pair + k
            out[pl.ds(row, 256, stride=16), :] = value[:, 128 * k : 128 * k + 128]

    copies[0].wait()
    for half in range(2):
        copies[1 + half].wait()
        for tile in range(2):
            stage(0, half, tile)
    for copy in copies[3:]:
        copy.wait()
    for first in range(2):
        for second in range(2):
            send(0, first, second)
            stage(1, first, second)
    for pair in range(2):
        for part in range(2):
            send(1, pair, part)


def across(left, right):
    return lax.dot_general(left, right, (((1,), (1,)), ((), ())), preferred_element_type=F32)


def straight(left, right):
    return lax.dot_general(left, right, (((1,), (0,)), ((), ())), preferred_element_type=F32)


def z_kernel(got, first_both, first_low, twist, second_all, out, field, high_q, low_q, image):
    lane = lax.broadcasted_iota(jnp.int32, (8, 128), 1)
    mode = lax.broadcasted_iota(jnp.int32, (8, 128), 0)
    weight = jnp.where((mode == 0) & (lane % 32 == 0), 0.5, 1.0).astype(F32)

    def first(slab, y, pair, slot):
        parts = []
        for part in range(2):
            blocks = []
            for k in range(2):
                row = slab * 1024 + 8 * part + 4 * y + 2 * pair + k
                head = got[pl.ds(row, 8, stride=16), :] * weight
                blocks.append(
                    jnp.concatenate([head, got[pl.ds(row + 128, 56, stride=16), :]], axis=0)
                )
            parts.append(jnp.concatenate(blocks, axis=1))
        high, low = split(jnp.concatenate(parts, axis=0))
        both = jnp.concatenate([high, low], axis=0)
        for part in range(2):
            half = pl.ds(64 * part, 64)
            other = pl.ds(128 + 64 * part, 64)
            re = straight(first_both[half], both) + straight(first_low[half], high)
            im = straight(first_both[other], both) + straight(first_low[other], high)
            c, s = twist[0, half], twist[1, half]
            for k in range(2):
                r, i = re[:, 128 * k : 128 * k + 128], im[:, 128 * k : 128 * k + 128]
                at = pl.ds(128 * k + 64 * part, 64)
                for column, value in enumerate((r * c - i * s, r * s + i * c)):
                    high_q[slot, at, pl.ds(128 * column, 128)], low_q[
                        slot, at, pl.ds(128 * column, 128)
                    ] = split(value)

    def second(slab, y, pair, slot):
        value = across(second_all[pl.ds(0, 128)], high_q[slot])
        value = value + across(second_all[pl.ds(128, 128)], high_q[slot])
        value = value + across(second_all[pl.ds(0, 128)], low_q[slot])
        for k in range(2):
            for near in range(4):
                field[4 * (2 * pair + k) + near, 2 * slab + y] = value[
                    32 * near : 32 * near + 32, 128 * k : 128 * k + 128
                ]

    first(0, 0, 0, 0)

    def transform(step, carry):
        slab, y = step // 2, step % 2
        after = jnp.minimum(step + 1, 7)
        first(slab, y, 1, 1)
        second(slab, y, 0, 0)
        first(after // 2, after % 2, 0, 0)
        second(slab, y, 1, 1)
        return carry

    lax.fori_loop(0, 8, transform, 0)

    def render(y, carry):
        before, after = (y + 7) % 8, (y + 1) % 8
        zero = jnp.zeros((32, 128), F32)
        clear, depth, total, tilted, glow = jnp.ones((32, 128), F32), zero, zero, zero, zero
        for x in range(16):
            half = field[x, y]
            shading = 2.0 + jnp.tanh(field[x, after] - field[x, before])
            square = half * half
            passed = jnp.exp2(square * (-4.0 * LOG2E / N))
            weight = (clear * shading) * (1.0 - passed)
            clear = clear * passed
            depth = depth + square
            total = total + weight
            tilted = tilted + weight * jnp.tanh(3.0 * half)
            glow = glow + weight * jnp.exp2(square * (-4.0 * LOG2E))
        red = 0.25 * (total + tilted)
        image[0, y] = red
        image[1, y] = 0.25 * glow
        image[2, y] = 0.5 * total - red
        image[3, y] = depth * (4.0 / N)
        return carry

    lax.fori_loop(0, 8, render, 0)
    first_half = lax.broadcasted_iota(jnp.int32, (32, 128), 1) < 64
    for slab in range(4):
        for channel in range(4):
            low, high = image[channel, 2 * slab], image[channel, 2 * slab + 1]
            mixed = (
                jnp.where(first_half, low, pltpu.roll(high, 64, 1)),
                jnp.where(first_half, pltpu.roll(low, 64, 1), high),
            )
            for core in range(2):
                out[pl.ds(slab * 256 + 4 * core + channel, 32, stride=8), :] = mixed[core]


def blend_kernel(got, out):
    depth = got[pl.ds(3, 256, stride=4), :]
    row = lax.broadcasted_iota(jnp.int32, (256, 256), 0)
    col = lax.broadcasted_iota(jnp.int32, (256, 256), 1)
    earlier = (col < row).astype(BF16)
    high = depth.astype(BF16)
    rest = depth - high.astype(F32)
    middle = rest.astype(BF16)
    low = (rest - middle.astype(F32)).astype(BF16)
    before = straight(earlier, high) + straight(earlier, middle) + straight(earlier, low)
    clear = jnp.exp(-before)
    rows = [
        jnp.sum(clear * got[pl.ds(channel, 256, stride=4), :], axis=0, keepdims=True)
        for channel in range(3)
    ]
    rows.append(1.0 - jnp.exp(-jnp.sum(depth, axis=0, keepdims=True)))
    for channel in range(4):
        for y in range(2):
            out[channel, pl.ds(y, 1), :] = rows[channel][:, 64 * y : 64 * y + 64]


def vmem_call(kernel, out_type, scratch=(), in_specs=None):
    params = pltpu.CompilerParams(vmem_limit_bytes=24 << 20)
    specs = {} if in_specs is None else {"in_specs": in_specs}
    return pl.pallas_call(
        kernel, out_shape=out_type, scratch_shapes=scratch, compiler_params=params, **specs
    )


def exchanged(blocks):
    got = lax.all_to_all(blocks, AXES, split_axis=0, concat_axis=0, tiled=True)
    return pltpu.with_memory_space_constraint(got.reshape(-1, 128), pltpu.VMEM)


def pinned(array):
    return pltpu.with_memory_space_constraint(array, pltpu.HBM)


def x_call(spectrum):
    tables = [pinned(jnp.asarray(table)) for table in x_tables()]
    far = pl.BlockSpec(memory_space=pltpu.HBM)
    lines = pltpu.VMEM((2, 512, 512), BF16)
    matrix = pltpu.VMEM((512, 512), BF16)
    return vmem_call(
        x_kernel,
        pltpu.VMEM((4096, 128), F32),
        [
            pltpu.VMEM((2, 2, 32, 4096), F32),
            pltpu.VMEM((32, 256), F32),
            matrix,
            matrix,
            lines,
            lines,
            pltpu.SemaphoreType.DMA((7,)),
        ],
        [far] * 4,
    )(pinned(spectrum), *tables)


def z_call(got):
    tables = [jnp.asarray(table) for table in z_tables()]
    lines = pltpu.VMEM((2, 256, 256), BF16)
    return vmem_call(
        z_kernel,
        pltpu.VMEM((1024, 128), F32),
        [pltpu.VMEM((16, 8, 32, 128), F32), lines, lines, pltpu.VMEM((4, 8, 32, 128), F32)],
    )(got, *tables)


def local(spectrum):
    got = exchanged(x_call(spectrum).reshape(256, 16, 128))
    got = exchanged(z_call(got).reshape(256, 4, 128))
    return vmem_call(blend_kernel, jax.ShapeDtypeStruct((4, 2, 64), F32))(got)


def solution(mesh):
    return jax.shard_map(
        local,
        mesh=mesh,
        in_specs=(P(None, "slab", "pencil", None),),
        out_specs=P(None, "slab", "pencil"),
        check_vma=False,
    )
```

```python
import math

import numpy as np

import jax
import jax.numpy as jnp
from jax import lax
from jax.experimental import pallas as pl
from jax.experimental.pallas import tpu as pltpu
from jax.sharding import PartitionSpec as P

N = 4096
LOG2E = math.log2(math.e)
AXES = ("slab", "pencil")
F32 = jnp.float32
BF16 = jnp.bfloat16


def split_np(table):
    high = table.astype(np.float32).astype(BF16)
    low = (table - high.astype(np.float64)).astype(np.float32).astype(BF16)
    return high, low


def split(value):
    high = value.astype(BF16)
    low = (value - high.astype(F32)).astype(BF16)
    return high, low


def complex_block(phase):
    cosine, sine = np.cos(phase), np.sin(phase)
    return np.block([[cosine, -sine], [sine, cosine]])


def x_tables():
    blocks = np.arange(256)
    matrix = complex_block(2 * np.pi * (blocks[:, None] * blocks[None, :] % 256) / 256)
    matrix = matrix.reshape(2, 256, 512).transpose(1, 0, 2).reshape(512, 512)
    fine = 2 * np.pi * (np.arange(16)[:, None] * blocks[None, :] % N) / N
    twist = np.stack([np.cos(fine), np.sin(fine)], axis=1).reshape(32, 256)
    return (twist.astype(np.float32),) + split_np(matrix)


def z_tables():
    outer = np.arange(128)[:, None] * np.arange(64)[None, :]
    first = complex_block(2 * np.pi * (outer % 128) / 128) / 4096
    fine = 2 * np.pi * (np.arange(128)[:, None] * (np.arange(128) % 32)[None, :] % N) / N
    twist = np.stack([np.cos(fine), np.sin(fine)])
    short = 2 * np.pi * (np.arange(32)[:, None] * np.arange(32)[None, :] % 32) / 32
    second = np.concatenate(
        [np.kron(np.eye(4), np.cos(short)), -np.kron(np.eye(4), np.sin(short))], axis=1
    )
    first = first.reshape(256, 2, 64).transpose(0, 2, 1).reshape(256, 128)
    first_high, first_low = split_np(first)
    first_both = np.concatenate([first_high, first_high], axis=1)
    second_all = np.concatenate(split_np(second), axis=0)
    return (first_both, first_low, twist.astype(np.float32), second_all)


def four(a, b, c, d):
    (ar, ai), (br, bi), (cr, ci), (dr, di) = a, b, c, d
    er, ei, fr, fi = ar + cr, ai + ci, ar - cr, ai - ci
    gr, gi, hr, hi = br + dr, bi + di, br - dr, bi - di
    return [(er + gr, ei + gi), (fr - hi, fi + hr), (er - gr, ei - gi), (fr + hi, fi - hr)]


def turned(value, steps):
    re, im = value
    if steps == 0:
        return value
    if steps == 4:
        return (-im, re)
    half = math.sqrt(0.5)
    if steps == 2:
        return ((re - im) * half, (re + im) * half)
    if steps == 6:
        return ((-re - im) * half, (re - im) * half)
    c, s = math.cos(math.pi * steps / 8), math.sin(math.pi * steps / 8)
    return (re * c - im * s, re * s + im * c)


def x_kernel(
    data, twist_hbm, high_hbm, low_hbm, out, cells_v, twist, high_w, low_w, high_t, low_t, sems
):
    copies = [pltpu.make_async_copy(twist_hbm, twist, sems.at[0])]
    for y in range(2):
        for half in range(2):
            rows = pl.ds(16 * half, 16)
            copies.append(
                pltpu.make_async_copy(
                    data.at[:, y, rows, :], cells_v.at[:, y, rows, :], sems.at[1 + 2 * y + half]
                )
            )
    copies.append(pltpu.make_async_copy(high_hbm, high_w, sems.at[5]))
    copies.append(pltpu.make_async_copy(low_hbm, low_w, sems.at[6]))
    for copy in copies:
        copy.start()

    def stage(y, half, tile):
        rows, lanes = pl.ds(16 * half, 16), pl.ds(128 * tile, 128)
        cells = [
            tuple(cells_v[part, y, rows, pl.ds(256 * t + 128 * tile, 128)] for part in range(2))
            for t in range(16)
        ]
        middle = [four(*(cells[4 * t1 + t0] for t1 in range(4))) for t0 in range(4)]
        for k1 in range(4):
            ends = four(*(turned(middle[t0][k1], t0 * k1) for t0 in range(4)))
            for k0 in range(4):
                fine = k1 + 4 * k0
                value = ends[k0]
                if fine:
                    re, im = value
                    c = twist[pl.ds(2 * fine, 1), lanes]
                    s = twist[pl.ds(2 * fine + 1, 1), lanes]
                    value = (re * c - im * s, re * s + im * c)
                for part in range(2):
                    high, low = split(value[part])
                    at = pl.ds(32 * fine + 16 * half, 16)
                    columns = pl.ds(256 * part + 128 * tile, 128)
                    high_t[y, at, columns] = high
                    low_t[y, at, columns] = low

    def send(y, pair):
        rows = pl.ds(256 * pair, 256)
        high, low = high_t[y, rows], low_t[y, rows]
        value = across(high_w[...], high) + across(low_w[...], high) + across(high_w[...], low)
        for k in range(2):
            out[pl.ds(4 * y + 2 * pair + k, 512, stride=8), :] = value[:, 128 * k : 128 * k + 128]

    copies[0].wait()
    for half in range(2):
        copies[1 + half].wait()
        for tile in range(2):
            stage(0, half, tile)
    for copy in copies[3:]:
        copy.wait()
    for pair in range(2):
        send(0, pair)
        for tile in range(2):
            stage(1, pair, tile)
    for pair in range(2):
        send(1, pair)


def across(left, right):
    return lax.dot_general(left, right, (((1,), (1,)), ((), ())), preferred_element_type=F32)


def straight(left, right):
    return lax.dot_general(left, right, (((1,), (0,)), ((), ())), preferred_element_type=F32)


def z_kernel(got, first_both, first_low, twist, second_all, out, field, high_q, low_q, image):
    lane = lax.broadcasted_iota(jnp.int32, (8, 128), 1)
    mode = lax.broadcasted_iota(jnp.int32, (8, 128), 0) // 2
    weight = jnp.where((mode == 0) & (lane % 32 == 0), 0.5, 1.0).astype(F32)

    def first(slab, y, pair, slot):
        blocks = []
        for k in range(2):
            row = slab * 1024 + 4 * y + 2 * pair + k
            head = got[pl.ds(row, 8, stride=8), :] * weight
            blocks.append(jnp.concatenate([head, got[pl.ds(row + 64, 120, stride=8), :]], axis=0))
        high, low = split(jnp.concatenate(blocks, axis=1))
        value = straight(first_both[...], jnp.concatenate([high, low], axis=0))
        value = value + straight(first_low[...], high)
        for part in range(2):
            half = pl.ds(64 * part, 64)
            c, s = twist[0, half], twist[1, half]
            for k in range(2):
                lanes = slice(128 * k, 128 * k + 128)
                r = value[64 * part : 64 * part + 64, lanes]
                i = value[128 + 64 * part : 192 + 64 * part, lanes]
                at = pl.ds(128 * k + 64 * part, 64)
                for column, turned_value in enumerate((r * c - i * s, r * s + i * c)):
                    columns = pl.ds(128 * column, 128)
                    high, low = split(turned_value)
                    high_q[slot, at, columns] = high
                    low_q[slot, at, columns] = low

    def second(slab, y, pair, slot):
        both = across(second_all[...], high_q[slot])
        value = both[:128] + both[128:] + across(second_all[pl.ds(0, 128)], low_q[slot])
        for k in range(2):
            for near in range(4):
                field[4 * (2 * pair + k) + near, 2 * slab + y] = value[
                    32 * near : 32 * near + 32, 128 * k : 128 * k + 128
                ]

    for pair in range(2):
        first(0, 0, pair, pair)

    def transform(slab, carry):
        after = jnp.minimum(slab + 1, 3)
        for y in range(2):
            for pair in range(2):
                first(slab if y == 0 else after, 1 - y, pair, 2 - 2 * y + pair)
                second(slab, y, pair, 2 * y + pair)
        return carry

    lax.fori_loop(0, 4, transform, 0, unroll=True)

    def render(y, carry):
        before, after = (y + 7) % 8, (y + 1) % 8
        zero = jnp.zeros((32, 128), F32)
        clear, depth, total, tilted, glow = jnp.ones((32, 128), F32), zero, zero, zero, zero
        for x in range(16):
            half = field[x, y]
            shading = 2.0 + jnp.tanh(field[x, after] - field[x, before])
            square = half * half
            passed = jnp.exp2(square * (-4.0 * LOG2E / N))
            weight = (clear * shading) * (1.0 - passed)
            clear = clear * passed
            depth = depth + square
            total = total + weight
            tilted = tilted + weight * jnp.tanh(3.0 * half)
            glow = glow + weight * jnp.exp2(square * (-4.0 * LOG2E))
        red = 0.25 * (total + tilted)
        image[0, y] = red
        image[1, y] = 0.25 * glow
        image[2, y] = 0.5 * total - red
        image[3, y] = depth * (4.0 / N)
        return carry

    lax.fori_loop(0, 8, render, 0)
    first_half = lax.broadcasted_iota(jnp.int32, (32, 128), 1) < 64
    for slab in range(4):
        for channel in range(4):
            low, high = image[channel, 2 * slab], image[channel, 2 * slab + 1]
            mixed = (
                jnp.where(first_half, low, pltpu.roll(high, 64, 1)),
                jnp.where(first_half, pltpu.roll(low, 64, 1), high),
            )
            for core in range(2):
                out[pl.ds(slab * 256 + 4 * core + channel, 32, stride=8), :] = mixed[core]


def blend_kernel(got, out):
    depth = got[pl.ds(3, 256, stride=4), :]
    row = lax.broadcasted_iota(jnp.int32, (256, 256), 0)
    col = lax.broadcasted_iota(jnp.int32, (256, 256), 1)
    earlier = (col < row).astype(BF16)
    high = depth.astype(BF16)
    rest = depth - high.astype(F32)
    middle = rest.astype(BF16)
    low = (rest - middle.astype(F32)).astype(BF16)
    before = straight(earlier, high) + straight(earlier, middle) + straight(earlier, low)
    clear = jnp.exp(-before)
    rows = [
        jnp.sum(clear * got[pl.ds(channel, 256, stride=4), :], axis=0, keepdims=True)
        for channel in range(3)
    ]
    rows.append(1.0 - jnp.exp(-jnp.sum(depth, axis=0, keepdims=True)))
    for channel in range(4):
        for y in range(2):
            out[channel, pl.ds(y, 1), :] = rows[channel][:, 64 * y : 64 * y + 64]


def vmem_call(kernel, out_type, scratch=(), in_specs=None):
    params = pltpu.CompilerParams(vmem_limit_bytes=24 << 20)
    specs = {} if in_specs is None else {"in_specs": in_specs}
    return pl.pallas_call(
        kernel, out_shape=out_type, scratch_shapes=scratch, compiler_params=params, **specs
    )


def exchanged(blocks):
    got = lax.all_to_all(blocks, AXES, split_axis=0, concat_axis=0, tiled=True)
    return pltpu.with_memory_space_constraint(got.reshape(-1, 128), pltpu.VMEM)


def pinned(array):
    return pltpu.with_memory_space_constraint(array, pltpu.HBM)


def x_call(spectrum):
    tables = [pinned(jnp.asarray(table)) for table in x_tables()]
    far = pl.BlockSpec(memory_space=pltpu.HBM)
    lines = pltpu.VMEM((2, 512, 512), BF16)
    matrix = pltpu.VMEM((512, 512), BF16)
    return vmem_call(
        x_kernel,
        pltpu.VMEM((4096, 128), F32),
        [
            pltpu.VMEM((2, 2, 32, 4096), F32),
            pltpu.VMEM((32, 256), F32),
            matrix,
            matrix,
            lines,
            lines,
            pltpu.SemaphoreType.DMA((7,)),
        ],
        [far] * 4,
    )(pinned(spectrum), *tables)


def z_call(got):
    tables = [jnp.asarray(table) for table in z_tables()]
    lines = pltpu.VMEM((4, 256, 256), BF16)
    return vmem_call(
        z_kernel,
        pltpu.VMEM((1024, 128), F32),
        [pltpu.VMEM((16, 8, 32, 128), F32), lines, lines, pltpu.VMEM((4, 8, 32, 128), F32)],
    )(got, *tables)


def local(spectrum):
    got = exchanged(x_call(spectrum).reshape(256, 16, 128))
    got = exchanged(z_call(got).reshape(256, 4, 128))
    return vmem_call(blend_kernel, jax.ShapeDtypeStruct((4, 2, 64), F32))(got)


def solution(mesh):
    return jax.shard_map(
        local,
        mesh=mesh,
        in_specs=(P(None, "slab", "pencil", None),),
        out_specs=P(None, "slab", "pencil"),
        check_vma=False,
    )
```

```python
import math

import numpy as np

import jax
import jax.numpy as jnp
from jax import lax
from jax.experimental import pallas as pl
from jax.experimental.pallas import tpu as pltpu
from jax.sharding import PartitionSpec as P

N = 4096
LOG2E = math.log2(math.e)
AXES = ("slab", "pencil")
F32 = jnp.float32
BF16 = jnp.bfloat16


def split_np(table):
    high = table.astype(np.float32).astype(BF16)
    low = (table - high.astype(np.float64)).astype(np.float32).astype(BF16)
    return high, low


def split(value):
    high = value.astype(BF16)
    low = (value - high.astype(F32)).astype(BF16)
    return high, low


def complex_block(phase):
    cosine, sine = np.cos(phase), np.sin(phase)
    return np.block([[cosine, -sine], [sine, cosine]])


def x_tables():
    lines = np.arange(256)
    phase = 2 * np.pi * ((2 * np.arange(128) + 1)[:, None] * lines[None, :] % 512) / 512
    cosine, sine = np.cos(phase), np.sin(phase)
    matrix = np.stack([[cosine, sine], [-sine, cosine]]).transpose(0, 2, 1, 3).reshape(512, 256)
    fine = 2 * np.pi * ((np.arange(16) - 8)[:, None] * lines[None, :] % N) / N
    twist = np.stack([np.cos(fine), np.sin(fine)], axis=1).reshape(32, 256)
    return (twist.astype(np.float32),) + split_np(matrix)


def z_tables():
    outer = np.arange(128)[:, None] * np.arange(64)[None, :]
    first = complex_block(2 * np.pi * (outer % 128) / 128) / 4096
    fine = 2 * np.pi * (np.arange(128)[:, None] * (np.arange(128) % 32)[None, :] % N) / N
    twist = np.stack([np.cos(fine), np.sin(fine)])
    short = 2 * np.pi * (np.arange(32)[:, None] * np.arange(32)[None, :] % 32) / 32
    second = np.concatenate(
        [np.kron(np.eye(4), np.cos(short)), -np.kron(np.eye(4), np.sin(short))], axis=1
    )
    first = first.reshape(256, 2, 64).transpose(0, 2, 1).reshape(256, 128)
    first = np.stack([first, first * np.where(np.arange(128) % 2, -1.0, 1.0)])
    first_high, first_low = split_np(first)
    first_both = np.concatenate([first_high, first_high], axis=2)
    second_all = np.concatenate(split_np(second), axis=0)
    return (first_both, first_low, twist.astype(np.float32), second_all)


def four(a, b, c, d):
    (ar, ai), (br, bi), (cr, ci), (dr, di) = a, b, c, d
    er, ei, fr, fi = ar + cr, ai + ci, ar - cr, ai - ci
    gr, gi, hr, hi = br + dr, bi + di, br - dr, bi - di
    return [(er + gr, ei + gi), (fr - hi, fi + hr), (er - gr, ei - gi), (fr + hi, fi - hr)]


def turned(value, steps):
    re, im = value
    if steps == 0:
        return value
    if steps == 4:
        return (-im, re)
    half = math.sqrt(0.5)
    if steps == 2:
        return ((re - im) * half, (re + im) * half)
    if steps == 6:
        return ((-re - im) * half, (re - im) * half)
    c, s = math.cos(math.pi * steps / 8), math.sin(math.pi * steps / 8)
    return (re * c - im * s, re * s + im * c)


def x_kernel(
    data, twist_hbm, high_hbm, low_hbm, out, cells_v, twist, high_w, low_w, high_t, low_t, sems
):
    copies = [pltpu.make_async_copy(twist_hbm, twist, sems.at[0])]
    for y in range(2):
        for half in range(2):
            rows = pl.ds(16 * half, 16)
            copies.append(
                pltpu.make_async_copy(
                    data.at[:, y, rows, :], cells_v.at[:, y, rows, :], sems.at[1 + 2 * y + half]
                )
            )
    copies.append(pltpu.make_async_copy(high_hbm, high_w, sems.at[5]))
    copies.append(pltpu.make_async_copy(low_hbm, low_w, sems.at[6]))
    for copy in copies:
        copy.start()

    def stage(y, half, tile):
        rows, lanes = pl.ds(16 * half, 16), pl.ds(128 * tile, 128)
        cells = [
            tuple(cells_v[part, y, rows, pl.ds(256 * t + 128 * tile, 128)] for part in range(2))
            for t in range(16)
        ]
        middle = [four(*(cells[4 * t1 + t0] for t1 in range(4))) for t0 in range(4)]
        for k1 in range(4):
            ends = four(*(turned(middle[t0][k1], t0 * k1) for t0 in range(4)))
            for k0 in range(4):
                fine = k1 + 4 * k0
                value = ends[k0]
                if fine != 8:
                    re, im = value
                    c = twist[pl.ds(2 * fine, 1), lanes]
                    s = twist[pl.ds(2 * fine + 1, 1), lanes]
                    value = (re * c - im * s, re * s + im * c)
                for part in range(2):
                    high, low = split(value[part])
                    at = pl.ds(32 * fine + 16 * half, 16)
                    columns = pl.ds(256 * part + 128 * tile, 128)
                    high_t[y, at, columns] = high
                    low_t[y, at, columns] = low

    def send(y, pair):
        rows = pl.ds(256 * pair, 256)
        parts = []
        for part in range(2):
            at = pl.ds(256 * part, 256)
            high, low = high_t[y, rows, at], low_t[y, rows, at]
            value = across(high_w[at], high) + across(low_w[at], high) + across(high_w[at], low)
            parts.append(value)
        for side, value in enumerate((parts[0] + parts[1], parts[0] - parts[1])):
            for k in range(2):
                at = pl.ds(2048 * side + 4 * y + 2 * pair + k, 256, stride=8)
                out[at, :] = value[:, 128 * k : 128 * k + 128]

    copies[0].wait()
    for half in range(2):
        copies[1 + half].wait()
        for tile in range(2):
            stage(0, half, tile)
    for copy in copies[3:]:
        copy.wait()
    for pair in range(2):
        send(0, pair)
        for tile in range(2):
            stage(1, pair, tile)
    for pair in range(2):
        send(1, pair)


def across(left, right):
    return lax.dot_general(left, right, (((1,), (1,)), ((), ())), preferred_element_type=F32)


def straight(left, right):
    return lax.dot_general(left, right, (((1,), (0,)), ((), ())), preferred_element_type=F32)


def z_kernel(
    got, first_both, first_low, twist, second_all, keep, give, field, high_q, low_q, image
):
    mirrored = lax.axis_index("slab") // 2
    core = lax.axis_index("pencil") % 2
    lane = lax.broadcasted_iota(jnp.int32, (8, 128), 1)
    mode = lax.broadcasted_iota(jnp.int32, (8, 128), 0) // 2
    weight = jnp.where((mode == 0) & (lane % 32 == 0), 0.5, 1.0).astype(F32)

    def first(slab, y, pair, slot):
        blocks = []
        for k in range(2):
            row = slab * 1024 + 4 * y + 2 * pair + k
            head = got[pl.ds(row, 8, stride=8), :] * weight
            blocks.append(jnp.concatenate([head, got[pl.ds(row + 64, 120, stride=8), :]], axis=0))
        high, low = split(jnp.concatenate(blocks, axis=1))
        value = straight(first_both[mirrored], jnp.concatenate([high, low], axis=0))
        value = value + straight(first_low[mirrored], high)
        for part in range(2):
            half = pl.ds(64 * part, 64)
            c, s = twist[0, half], twist[1, half]
            for k in range(2):
                lanes = slice(128 * k, 128 * k + 128)
                r = value[64 * part : 64 * part + 64, lanes]
                i = value[128 + 64 * part : 192 + 64 * part, lanes]
                at = pl.ds(128 * k + 64 * part, 64)
                for column, turned_value in enumerate((r * c - i * s, r * s + i * c)):
                    columns = pl.ds(128 * column, 128)
                    high, low = split(turned_value)
                    high_q[slot, at, columns] = high
                    low_q[slot, at, columns] = low

    def second(slab, y, pair, slot):
        both = across(second_all[...], high_q[slot])
        value = both[:128] + both[128:] + across(second_all[pl.ds(0, 128)], low_q[slot])
        for k in range(2):
            for near in range(4):
                field[4 * (2 * pair + k) + near, 2 * slab + y] = value[
                    32 * near : 32 * near + 32, 128 * k : 128 * k + 128
                ]

    for pair in range(2):
        first(0, 0, pair, pair)

    def transform(slab, carry):
        after = jnp.minimum(slab + 1, 3)
        for y in range(2):
            for pair in range(2):
                first(slab if y == 0 else after, 1 - y, pair, 2 - 2 * y + pair)
                second(slab, y, pair, 2 * y + pair)
        return carry

    lax.fori_loop(0, 4, transform, 0, unroll=True)

    def render(y, carry):
        before, after = (y + 7) % 8, (y + 1) % 8
        zero = jnp.zeros((32, 128), F32)
        clear, depth, total, tilted, glow = jnp.ones((32, 128), F32), zero, zero, zero, zero
        for x in range(16):
            half = field[x, y]
            shading = 2.0 + jnp.tanh(field[x, after] - field[x, before])
            square = half * half
            passed = jnp.exp2(square * (-4.0 * LOG2E / N))
            weight = (clear * shading) * (1.0 - passed)
            clear = clear * passed
            depth = depth + square
            total = total + weight
            tilted = tilted + weight * jnp.tanh(3.0 * half)
            glow = glow + weight * jnp.exp2(square * (-4.0 * LOG2E))
        red = 0.25 * (total + tilted)
        image[0, y] = red
        image[1, y] = 0.25 * glow
        image[2, y] = 0.5 * total - red
        image[3, y] = depth * (4.0 / N)
        return carry

    lax.fori_loop(0, 8, render, 0)
    first_half = lax.broadcasted_iota(jnp.int32, (32, 128), 1) < 64
    for slab in range(4):
        for channel in range(4):
            low, high = image[channel, 2 * slab], image[channel, 2 * slab + 1]
            mixed = (
                jnp.where(first_half, low, pltpu.roll(high, 64, 1)),
                jnp.where(first_half, pltpu.roll(low, 64, 1), high),
            )
            at = pl.ds(32 * (4 * channel + slab), 32)
            keep[at, :] = jnp.where(core == 0, mixed[0], mixed[1])
            give[at, :] = jnp.where(core == 0, mixed[1], mixed[0])


def pair_kernel(keep, got, out):
    own_first = lax.axis_index("pencil") % 2 == lax.axis_index("slab") // 2
    for slab in range(4):
        own = [keep[pl.ds(32 * (4 * channel + slab), 32), :] for channel in range(4)]
        other = [got[pl.ds(32 * (4 * channel + slab), 32), :] for channel in range(4)]
        clear = jnp.exp(-jnp.where(own_first, own[3], other[3]))
        for channel in range(4):
            if channel == 3:
                value = own[3] + other[3]
            else:
                front = jnp.where(own_first, own[channel], other[channel])
                back = jnp.where(own_first, other[channel], own[channel])
                value = front + clear * back
            out[pl.ds(128 * slab + channel, 32, stride=4), :] = value


def blend_kernel(got, out):
    depth = got[pl.ds(3, 128, stride=4), :]
    row = lax.broadcasted_iota(jnp.int32, (128, 128), 0)
    col = lax.broadcasted_iota(jnp.int32, (128, 128), 1)
    rank = jnp.where(row < 64, row, 191 - row)
    earlier = (jnp.where(col < 64, col, 191 - col) < rank).astype(BF16)
    high = depth.astype(BF16)
    rest = depth - high.astype(F32)
    middle = rest.astype(BF16)
    low = (rest - middle.astype(F32)).astype(BF16)
    before = straight(earlier, high) + straight(earlier, middle) + straight(earlier, low)
    clear = jnp.exp(-before)
    rows = [
        jnp.sum(clear * got[pl.ds(channel, 128, stride=4), :], axis=0, keepdims=True)
        for channel in range(3)
    ]
    rows.append(1.0 - jnp.exp(-jnp.sum(depth, axis=0, keepdims=True)))
    for channel in range(4):
        for y in range(2):
            out[channel, pl.ds(y, 1), :] = rows[channel][:, 64 * y : 64 * y + 64]


def vmem_call(kernel, out_type, scratch=(), in_specs=None):
    params = pltpu.CompilerParams(vmem_limit_bytes=24 << 20)
    specs = {} if in_specs is None else {"in_specs": in_specs}
    return pl.pallas_call(
        kernel, out_shape=out_type, scratch_shapes=scratch, compiler_params=params, **specs
    )


def near(array):
    return pltpu.with_memory_space_constraint(array, pltpu.VMEM)


def pinned(array):
    return pltpu.with_memory_space_constraint(array, pltpu.HBM)


def x_call(spectrum):
    tables = [pinned(jnp.asarray(table)) for table in x_tables()]
    far = pl.BlockSpec(memory_space=pltpu.HBM)
    lines = pltpu.VMEM((2, 512, 512), BF16)
    matrix = pltpu.VMEM((512, 256), BF16)
    return vmem_call(
        x_kernel,
        pltpu.VMEM((4096, 128), F32),
        [
            pltpu.VMEM((2, 2, 32, 4096), F32),
            pltpu.VMEM((32, 256), F32),
            matrix,
            matrix,
            lines,
            lines,
            pltpu.SemaphoreType.DMA((7,)),
        ],
        [far] * 4,
    )(pinned(spectrum), *tables)


def z_call(got):
    tables = [jnp.asarray(table) for table in z_tables()]
    lines = pltpu.VMEM((4, 256, 256), BF16)
    return vmem_call(
        z_kernel,
        (pltpu.VMEM((512, 128), F32), pltpu.VMEM((512, 128), F32)),
        [pltpu.VMEM((16, 8, 32, 128), F32), lines, lines, pltpu.VMEM((4, 8, 32, 128), F32)],
    )(got, *tables)


def local(spectrum):
    blocks = x_call(spectrum).reshape(256, 16, 128)
    got = lax.all_to_all(blocks, AXES, split_axis=0, concat_axis=0, tiled=True)
    keep, give = z_call(near(got.reshape(4096, 128)))
    swap = [(i, i ^ 1) for i in range(lax.axis_size("pencil"))]
    other = near(lax.ppermute(give, "pencil", swap))
    blocks = vmem_call(pair_kernel, pltpu.VMEM((512, 128), F32))(near(keep), other)
    same_core = [[2 * i + core for i in range(128)] for core in range(2)]
    got = lax.all_to_all(
        blocks.reshape(128, 4, 128),
        AXES,
        split_axis=0,
        concat_axis=0,
        axis_index_groups=same_core,
        tiled=True,
    )
    out_type = jax.ShapeDtypeStruct((4, 2, 64), F32)
    return vmem_call(blend_kernel, out_type)(near(got.reshape(512, 128)))


def solution(mesh):
    return jax.shard_map(
        local,
        mesh=mesh,
        in_specs=(P(None, "slab", "pencil", None),),
        out_specs=P(None, "slab", "pencil"),
        check_vma=False,
    )
```

```python
import math

import numpy as np

import jax
import jax.numpy as jnp
from jax import lax
from jax.experimental import pallas as pl
from jax.experimental.pallas import tpu as pltpu
from jax.sharding import PartitionSpec as P

N = 4096
LOG2E = math.log2(math.e)
AXES = ("slab", "pencil")
F32 = jnp.float32
BF16 = jnp.bfloat16


def split_np(table):
    high = table.astype(np.float32).astype(BF16)
    low = (table - high.astype(np.float64)).astype(np.float32).astype(BF16)
    return high, low


def split(value):
    high = value.astype(BF16)
    low = (value - high.astype(F32)).astype(BF16)
    return high, low


def complex_block(phase):
    cosine, sine = np.cos(phase), np.sin(phase)
    return np.block([[cosine, -sine], [sine, cosine]])


def x_tables():
    lines = np.arange(256)
    phase = 2 * np.pi * ((2 * np.arange(128) + 1)[:, None] * lines[None, :] % 512) / 512
    cosine, sine = np.cos(phase), np.sin(phase)
    matrix = np.stack([[cosine, sine], [-sine, cosine]]).transpose(0, 2, 1, 3).reshape(512, 256)
    fine = 2 * np.pi * ((np.arange(16) - 8)[:, None] * lines[None, :] % N) / N
    twist = np.stack([np.cos(fine), np.sin(fine)], axis=1).reshape(32, 256)
    return (twist.astype(np.float32),) + split_np(matrix)


def z_tables():
    outer = np.arange(128)[:, None] * np.arange(64)[None, :]
    first = complex_block(2 * np.pi * (outer % 128) / 128) / 4096
    fine = 2 * np.pi * (np.arange(128)[:, None] * (np.arange(128) % 32)[None, :] % N) / N
    twist = np.stack([np.cos(fine), np.sin(fine)])
    short = 2 * np.pi * (np.arange(32)[:, None] * np.arange(32)[None, :] % 32) / 32
    second = np.concatenate(
        [np.kron(np.eye(4), np.cos(short)), -np.kron(np.eye(4), np.sin(short))], axis=1
    )
    first = first.reshape(256, 2, 64).transpose(0, 2, 1).reshape(256, 128)
    first = np.stack([first, first * np.where(np.arange(128) % 2, -1.0, 1.0)])
    first_high, first_low = split_np(first)
    first_both = np.concatenate([first_high, first_high], axis=2)
    second_all = np.concatenate(split_np(second), axis=0)
    return (first_both, first_low, twist.astype(np.float32), second_all)


def four(a, b, c, d):
    (ar, ai), (br, bi), (cr, ci), (dr, di) = a, b, c, d
    er, ei, fr, fi = ar + cr, ai + ci, ar - cr, ai - ci
    gr, gi, hr, hi = br + dr, bi + di, br - dr, bi - di
    return [(er + gr, ei + gi), (fr - hi, fi + hr), (er - gr, ei - gi), (fr + hi, fi - hr)]


def turned(value, steps):
    re, im = value
    if steps == 0:
        return value
    if steps == 4:
        return (-im, re)
    half = math.sqrt(0.5)
    if steps == 2:
        return ((re - im) * half, (re + im) * half)
    if steps == 6:
        return ((-re - im) * half, (re - im) * half)
    c, s = math.cos(math.pi * steps / 8), math.sin(math.pi * steps / 8)
    return (re * c - im * s, re * s + im * c)


def x_kernel(
    data, twist_hbm, high_hbm, low_hbm, out, cells_v, twist, high_w, low_w, high_t, low_t, sems
):
    copies = [pltpu.make_async_copy(twist_hbm, twist, sems.at[0])]
    for y in range(2):
        for half in range(2):
            rows = pl.ds(16 * half, 16)
            copies.append(
                pltpu.make_async_copy(
                    data.at[:, y, rows, :], cells_v.at[:, y, rows, :], sems.at[1 + 2 * y + half]
                )
            )
    copies.append(pltpu.make_async_copy(high_hbm, high_w, sems.at[5]))
    copies.append(pltpu.make_async_copy(low_hbm, low_w, sems.at[6]))
    for copy in copies:
        copy.start()

    def stage(y, half, tile):
        rows, lanes = pl.ds(16 * half, 16), pl.ds(128 * tile, 128)
        cells = [
            tuple(cells_v[part, y, rows, pl.ds(256 * t + 128 * tile, 128)] for part in range(2))
            for t in range(16)
        ]
        middle = [four(*(cells[4 * t1 + t0] for t1 in range(4))) for t0 in range(4)]
        for k1 in range(4):
            ends = four(*(turned(middle[t0][k1], t0 * k1) for t0 in range(4)))
            for k0 in range(4):
                fine = k1 + 4 * k0
                value = ends[k0]
                if fine != 8:
                    re, im = value
                    c = twist[pl.ds(2 * fine, 1), lanes]
                    s = twist[pl.ds(2 * fine + 1, 1), lanes]
                    value = (re * c - im * s, re * s + im * c)
                for part in range(2):
                    high, low = split(value[part])
                    at = pl.ds(32 * fine + 16 * half, 16)
                    columns = pl.ds(256 * part + 128 * tile, 128)
                    high_t[y, at, columns] = high
                    low_t[y, at, columns] = low

    def send(y, pair):
        rows = pl.ds(256 * pair, 256)
        parts = []
        for part in range(2):
            at = pl.ds(256 * part, 256)
            high, low = high_t[y, rows, at], low_t[y, rows, at]
            value = across(high_w[at], high) + across(low_w[at], high) + across(high_w[at], low)
            parts.append(value)
        for side, value in enumerate((parts[0] + parts[1], parts[0] - parts[1])):
            for k in range(2):
                at = pl.ds(2048 * side + 4 * y + 2 * pair + k, 256, stride=8)
                out[at, :] = value[:, 128 * k : 128 * k + 128]

    copies[0].wait()
    for half in range(2):
        copies[1 + half].wait()
        for tile in range(2):
            stage(0, half, tile)
    for copy in copies[3:]:
        copy.wait()
    for pair in range(2):
        send(0, pair)
        for tile in range(2):
            stage(1, pair, tile)
    for pair in range(2):
        send(1, pair)


def across(left, right):
    return lax.dot_general(left, right, (((1,), (1,)), ((), ())), preferred_element_type=F32)


def straight(left, right):
    return lax.dot_general(left, right, (((1,), (0,)), ((), ())), preferred_element_type=F32)


def z_kernel(
    got, first_both, first_low, twist, second_all, keep, give, field, high_q, low_q, image
):
    mirrored = lax.axis_index("slab") // 2
    core = lax.axis_index("pencil") % 2
    lane = lax.broadcasted_iota(jnp.int32, (8, 128), 1)
    mode = lax.broadcasted_iota(jnp.int32, (8, 128), 0) // 2
    weight = jnp.where((mode == 0) & (lane % 32 == 0), 0.5, 1.0).astype(F32)

    def first(slab, y, pair, slot):
        blocks = []
        for k in range(2):
            row = slab * 1024 + 4 * y + 2 * pair + k
            head = got[pl.ds(row, 8, stride=8), :] * weight
            blocks.append(jnp.concatenate([head, got[pl.ds(row + 64, 120, stride=8), :]], axis=0))
        high, low = split(jnp.concatenate(blocks, axis=1))
        value = straight(first_both[mirrored], jnp.concatenate([high, low], axis=0))
        value = value + straight(first_low[mirrored], high)
        for part in range(2):
            half = pl.ds(64 * part, 64)
            c, s = twist[0, half], twist[1, half]
            for k in range(2):
                lanes = slice(128 * k, 128 * k + 128)
                r = value[64 * part : 64 * part + 64, lanes]
                i = value[128 + 64 * part : 192 + 64 * part, lanes]
                at = pl.ds(128 * k + 64 * part, 64)
                for column, turned_value in enumerate((r * c - i * s, r * s + i * c)):
                    columns = pl.ds(128 * column, 128)
                    high, low = split(turned_value)
                    high_q[slot, at, columns] = high
                    low_q[slot, at, columns] = low

    def second(slab, y, pair, slot):
        both = across(second_all[...], high_q[slot])
        value = both[:128] + both[128:] + across(second_all[pl.ds(0, 128)], low_q[slot])
        for k in range(2):
            for near in range(4):
                field[4 * (2 * pair + k) + near, 2 * slab + y] = value[
                    32 * near : 32 * near + 32, 128 * k : 128 * k + 128
                ]

    first_half = lax.broadcasted_iota(jnp.int32, (32, 128), 1) < 64

    def render(y, part):
        rows = pl.ds(16 * part, 16)
        before, after = (y + 7) % 8, (y + 1) % 8
        zero = jnp.zeros((16, 128), F32)
        clear, depth, total, tilted, glow = jnp.ones((16, 128), F32), zero, zero, zero, zero
        for x in range(16):
            half = field[x, y, rows]
            shading = 2.0 + jnp.tanh(field[x, after, rows] - field[x, before, rows])
            square = half * half
            passed = clear * jnp.exp2(square * (-4.0 * LOG2E / N))
            weight = (clear - passed) * shading
            clear = passed
            depth = depth + square
            total = total + weight
            tilted = tilted + weight * jnp.tanh(3.0 * half)
            glow = glow + weight * jnp.exp2(square * (-4.0 * LOG2E))
        red = 0.25 * (total + tilted)
        image[0, y, rows] = red
        image[1, y, rows] = 0.25 * glow
        image[2, y, rows] = 0.5 * total - red
        image[3, y, rows] = depth * (4.0 / N)

    def pack(slab):
        for channel in range(4):
            low, high = image[channel, 2 * slab], image[channel, 2 * slab + 1]
            mixed = (
                jnp.where(first_half, low, pltpu.roll(high, 64, 1)),
                jnp.where(first_half, pltpu.roll(low, 64, 1), high),
            )
            at = pl.ds(32 * (4 * channel + slab), 32)
            keep[at, :] = jnp.where(core == 0, mixed[0], mixed[1])
            give[at, :] = jnp.where(core == 0, mixed[1], mixed[0])

    order = (7, 0, 1, 2, 3, 4, 5, 6)
    for pair in range(2):
        first(order[0] // 2, order[0] % 2, pair, pair)
    for step in range(8):
        for pair in range(2):
            if step < 7:
                y = order[step + 1]
                first(y // 2, y % 2, pair, 2 - 2 * (step % 2) + pair)
            y = order[step]
            second(y // 2, y % 2, pair, 2 * (step % 2) + pair)
            if step >= 3:
                render(step - 3, pair)
        if step in (4, 6):
            pack(step // 2 - 2)
    for y in (5, 6, 7):
        for part in range(2):
            render(y, part)
        if y != 6:
            pack(y // 2)


def pair_kernel(keep, got, out):
    own_first = lax.axis_index("pencil") % 2 == lax.axis_index("slab") // 2
    for slab in range(4):
        own = [keep[pl.ds(32 * (4 * channel + slab), 32), :] for channel in range(4)]
        other = [got[pl.ds(32 * (4 * channel + slab), 32), :] for channel in range(4)]
        clear = jnp.exp(-jnp.where(own_first, own[3], other[3]))
        for channel in range(4):
            if channel == 3:
                value = own[3] + other[3]
            else:
                front = jnp.where(own_first, own[channel], other[channel])
                back = jnp.where(own_first, other[channel], own[channel])
                value = front + clear * back
            out[pl.ds(128 * slab + channel, 32, stride=4), :] = value


def blend_kernel(got, out):
    depth = got[pl.ds(3, 128, stride=4), :]
    row = lax.broadcasted_iota(jnp.int32, (128, 128), 0)
    col = lax.broadcasted_iota(jnp.int32, (128, 128), 1)
    rank = jnp.where(row < 64, row, 191 - row)
    earlier = (jnp.where(col < 64, col, 191 - col) < rank).astype(BF16)
    high = depth.astype(BF16)
    rest = depth - high.astype(F32)
    middle = rest.astype(BF16)
    low = (rest - middle.astype(F32)).astype(BF16)
    before = straight(earlier, high) + straight(earlier, middle) + straight(earlier, low)
    clear = jnp.exp(-before)
    rows = [
        jnp.sum(clear * got[pl.ds(channel, 128, stride=4), :], axis=0, keepdims=True)
        for channel in range(3)
    ]
    rows.append(1.0 - jnp.exp(-jnp.sum(depth, axis=0, keepdims=True)))
    for channel in range(4):
        for y in range(2):
            out[channel, pl.ds(y, 1), :] = rows[channel][:, 64 * y : 64 * y + 64]


def vmem_call(kernel, out_type, scratch=(), in_specs=None):
    params = pltpu.CompilerParams(vmem_limit_bytes=24 << 20)
    specs = {} if in_specs is None else {"in_specs": in_specs}
    return pl.pallas_call(
        kernel, out_shape=out_type, scratch_shapes=scratch, compiler_params=params, **specs
    )


def near(array):
    return pltpu.with_memory_space_constraint(array, pltpu.VMEM)


def pinned(array):
    return pltpu.with_memory_space_constraint(array, pltpu.HBM)


def x_call(spectrum):
    tables = [pinned(jnp.asarray(table)) for table in x_tables()]
    far = pl.BlockSpec(memory_space=pltpu.HBM)
    lines = pltpu.VMEM((2, 512, 512), BF16)
    matrix = pltpu.VMEM((512, 256), BF16)
    return vmem_call(
        x_kernel,
        pltpu.VMEM((4096, 128), F32),
        [
            pltpu.VMEM((2, 2, 32, 4096), F32),
            pltpu.VMEM((32, 256), F32),
            matrix,
            matrix,
            lines,
            lines,
            pltpu.SemaphoreType.DMA((7,)),
        ],
        [far] * 4,
    )(pinned(spectrum), *tables)


def z_call(got):
    tables = [jnp.asarray(table) for table in z_tables()]
    lines = pltpu.VMEM((4, 256, 256), BF16)
    return vmem_call(
        z_kernel,
        (pltpu.VMEM((512, 128), F32), pltpu.VMEM((512, 128), F32)),
        [pltpu.VMEM((16, 8, 32, 128), F32), lines, lines, pltpu.VMEM((4, 8, 32, 128), F32)],
    )(got, *tables)


def local(spectrum):
    blocks = x_call(spectrum).reshape(256, 16, 128)
    got = lax.all_to_all(blocks, AXES, split_axis=0, concat_axis=0, tiled=True)
    keep, give = z_call(near(got.reshape(4096, 128)))
    swap = [(i, i ^ 1) for i in range(lax.axis_size("pencil"))]
    other = near(lax.ppermute(give, "pencil", swap))
    blocks = vmem_call(pair_kernel, pltpu.VMEM((512, 128), F32))(near(keep), other)
    same_core = [[2 * i + core for i in range(128)] for core in range(2)]
    got = lax.all_to_all(
        blocks.reshape(128, 4, 128),
        AXES,
        split_axis=0,
        concat_axis=0,
        axis_index_groups=same_core,
        tiled=True,
    )
    out_type = jax.ShapeDtypeStruct((4, 2, 64), F32)
    return vmem_call(blend_kernel, out_type)(near(got.reshape(512, 128)))


def solution(mesh):
    return jax.shard_map(
        local,
        mesh=mesh,
        in_specs=(P(None, "slab", "pencil", None),),
        out_specs=P(None, "slab", "pencil"),
        check_vma=False,
    )
```

```python
import math

import numpy as np

import jax
import jax.numpy as jnp
from jax import lax
from jax.experimental import pallas as pl
from jax.experimental.pallas import tpu as pltpu
from jax.sharding import PartitionSpec as P

N = 4096
LOG2E = math.log2(math.e)
AXES = ("slab", "pencil")
F32 = jnp.float32
BF16 = jnp.bfloat16


def split_np(table):
    high = table.astype(np.float32).astype(BF16)
    low = (table - high.astype(np.float64)).astype(np.float32).astype(BF16)
    return high, low


def split(value):
    high = value.astype(BF16)
    low = (value - high.astype(F32)).astype(BF16)
    return high, low


def complex_block(phase):
    cosine, sine = np.cos(phase), np.sin(phase)
    return np.block([[cosine, -sine], [sine, cosine]])


def x_tables():
    lines = np.arange(256)
    phase = 2 * np.pi * ((2 * np.arange(128) + 1)[:, None] * lines[None, :] % 512) / 512
    cosine, sine = np.cos(phase), np.sin(phase)
    matrix = np.stack([[cosine, sine], [-sine, cosine]]).transpose(0, 2, 1, 3).reshape(512, 256)
    fine = 2 * np.pi * ((np.arange(16) - 8)[:, None] * lines[None, :] % N) / N
    twist = np.stack([np.cos(fine), np.sin(fine)], axis=1).reshape(32, 256)
    return (twist.astype(np.float32),) + split_np(matrix)


def z_tables():
    outer = np.arange(128)[:, None] * np.arange(64)[None, :]
    first = complex_block(2 * np.pi * (outer % 128) / 128) / 4096
    fine = 2 * np.pi * (np.arange(128)[:, None] * (np.arange(128) % 32)[None, :] % N) / N
    twist = np.stack([np.cos(fine), np.sin(fine)])
    short = 2 * np.pi * (np.arange(32)[:, None] * np.arange(32)[None, :] % 32) / 32
    second = np.concatenate(
        [np.kron(np.eye(4), np.cos(short)), -np.kron(np.eye(4), np.sin(short))], axis=1
    )
    first = first.reshape(256, 2, 64).transpose(0, 2, 1).reshape(256, 128)
    first = np.stack([first, first * np.where(np.arange(128) % 2, -1.0, 1.0)])
    first_high, first_low = split_np(first)
    first_both = np.concatenate([first_high, first_high], axis=2)
    second_all = np.concatenate(split_np(second), axis=0)
    return (first_both, first_low, twist.astype(np.float32), second_all)


def four(a, b, c, d):
    (ar, ai), (br, bi), (cr, ci), (dr, di) = a, b, c, d
    er, ei, fr, fi = ar + cr, ai + ci, ar - cr, ai - ci
    gr, gi, hr, hi = br + dr, bi + di, br - dr, bi - di
    return [(er + gr, ei + gi), (fr - hi, fi + hr), (er - gr, ei - gi), (fr + hi, fi - hr)]


def turned(value, steps):
    re, im = value
    if steps == 0:
        return value
    if steps == 4:
        return (-im, re)
    half = math.sqrt(0.5)
    if steps == 2:
        return ((re - im) * half, (re + im) * half)
    if steps == 6:
        return ((-re - im) * half, (re - im) * half)
    c, s = math.cos(math.pi * steps / 8), math.sin(math.pi * steps / 8)
    return (re * c - im * s, re * s + im * c)


def x_kernel(
    data, twist_hbm, high_hbm, low_hbm, out, cells_v, twist, high_w, low_w, high_t, low_t, sems
):
    copies = [pltpu.make_async_copy(twist_hbm, twist, sems.at[0])]
    for y in range(2):
        for half in range(2):
            rows = pl.ds(16 * half, 16)
            copies.append(
                pltpu.make_async_copy(
                    data.at[:, y, rows, :], cells_v.at[:, y, rows, :], sems.at[1 + 2 * y + half]
                )
            )
    copies.append(pltpu.make_async_copy(high_hbm, high_w, sems.at[5]))
    copies.append(pltpu.make_async_copy(low_hbm, low_w, sems.at[6]))
    for copy in copies:
        copy.start()

    def stage(y, half, tile):
        rows, lanes = pl.ds(16 * half, 16), pl.ds(128 * tile, 128)
        cells = [
            tuple(cells_v[part, y, rows, pl.ds(256 * t + 128 * tile, 128)] for part in range(2))
            for t in range(16)
        ]
        middle = [four(*(cells[4 * t1 + t0] for t1 in range(4))) for t0 in range(4)]
        for k1 in range(4):
            ends = four(*(turned(middle[t0][k1], t0 * k1) for t0 in range(4)))
            for k0 in range(4):
                fine = k1 + 4 * k0
                value = ends[k0]
                if fine != 8:
                    re, im = value
                    c = twist[pl.ds(2 * fine, 1), lanes]
                    s = twist[pl.ds(2 * fine + 1, 1), lanes]
                    value = (re * c - im * s, re * s + im * c)
                for part in range(2):
                    high, low = split(value[part])
                    at = pl.ds(32 * fine + 16 * half, 16)
                    columns = pl.ds(256 * part + 128 * tile, 128)
                    high_t[y, at, columns] = high
                    low_t[y, at, columns] = low

    def send(y, pair):
        rows = pl.ds(256 * pair, 256)
        parts = []
        for part in range(2):
            at = pl.ds(256 * part, 256)
            high, low = high_t[y, rows, at], low_t[y, rows, at]
            value = across(high_w[at], high) + across(low_w[at], high) + across(high_w[at], low)
            parts.append(value)
        for side, value in enumerate((parts[0] + parts[1], parts[0] - parts[1])):
            for k in range(2):
                at = pl.ds(2048 * side + 4 * y + 2 * pair + k, 256, stride=8)
                out[at, :] = value[:, 128 * k : 128 * k + 128]

    copies[0].wait()
    for half in range(2):
        copies[1 + half].wait()
        for tile in range(2):
            stage(0, half, tile)
    for copy in copies[3:]:
        copy.wait()
    for pair in range(2):
        send(0, pair)
        for tile in range(2):
            stage(1, pair, tile)
    for pair in range(2):
        send(1, pair)


def across(left, right):
    return lax.dot_general(left, right, (((1,), (1,)), ((), ())), preferred_element_type=F32)


def straight(left, right):
    return lax.dot_general(left, right, (((1,), (0,)), ((), ())), preferred_element_type=F32)


def z_kernel(
    got, first_both, first_low, twist, second_all, keep, give, field, high_q, low_q, image
):
    mirrored = lax.axis_index("slab") // 2
    core = lax.axis_index("pencil") % 2
    lane = lax.broadcasted_iota(jnp.int32, (8, 128), 1)
    mode = lax.broadcasted_iota(jnp.int32, (8, 128), 0) // 2
    weight = jnp.where((mode == 0) & (lane % 32 == 0), 0.5, 1.0).astype(F32)

    def first(slab, y, pair, slot):
        blocks = []
        for k in range(2):
            row = slab * 1024 + 4 * y + 2 * pair + k
            head = got[pl.ds(row, 8, stride=8), :] * weight
            blocks.append(jnp.concatenate([head, got[pl.ds(row + 64, 120, stride=8), :]], axis=0))
        high, low = split(jnp.concatenate(blocks, axis=1))
        value = straight(first_both[mirrored], jnp.concatenate([high, low], axis=0))
        value = value + straight(first_low[mirrored], high)
        for part in range(2):
            half = pl.ds(64 * part, 64)
            c, s = twist[0, half], twist[1, half]
            for k in range(2):
                lanes = slice(128 * k, 128 * k + 128)
                r = value[64 * part : 64 * part + 64, lanes]
                i = value[128 + 64 * part : 192 + 64 * part, lanes]
                at = pl.ds(128 * k + 64 * part, 64)
                for column, turned_value in enumerate((r * c - i * s, r * s + i * c)):
                    columns = pl.ds(128 * column, 128)
                    high, low = split(turned_value)
                    high_q[slot, at, columns] = high
                    low_q[slot, at, columns] = low

    def second(slab, y, pair, slot):
        both = across(second_all[...], high_q[slot])
        value = both[:128] + both[128:] + across(second_all[pl.ds(0, 128)], low_q[slot])
        for k in range(2):
            for near in range(4):
                field[4 * (2 * pair + k) + near, 2 * slab + y] = value[
                    32 * near : 32 * near + 32, 128 * k : 128 * k + 128
                ]


    def render(y, part):
        rows = pl.ds(16 * part, 16)
        before, after = (y + 7) % 8, (y + 1) % 8
        zero = jnp.zeros((16, 128), F32)
        clear, depth, total, tilted, glow = jnp.ones((16, 128), F32), zero, zero, zero, zero
        for x in range(16):
            half = field[x, y, rows]
            shading = 2.0 + jnp.tanh(field[x, after, rows] - field[x, before, rows])
            square = half * half
            passed = clear * jnp.exp2(square * (-4.0 * LOG2E / N))
            weight = (clear - passed) * shading
            clear = passed
            depth = depth + square
            total = total + weight
            tilted = tilted + weight * jnp.tanh(3.0 * half)
            glow = glow + weight * jnp.exp2(square * (-4.0 * LOG2E))
        red = 0.25 * (total + tilted)
        image[0, y, rows] = red
        image[1, y, rows] = 0.25 * glow
        image[2, y, rows] = 0.5 * total - red
        image[3, y, rows] = depth * (4.0 / N)

    def pack(slab):
        for channel in range(4):
            at = pl.ds(32 * (4 * channel + slab), 32)
            keep[at, :] = image[channel, 2 * slab + core]
            give[at, :] = image[channel, 2 * slab + 1 - core]

    order = (7, 0, 1, 2, 3, 4, 5, 6)
    for pair in range(2):
        first(order[0] // 2, order[0] % 2, pair, pair)
    for step in range(8):
        for pair in range(2):
            if step < 7:
                y = order[step + 1]
                first(y // 2, y % 2, pair, 2 - 2 * (step % 2) + pair)
            y = order[step]
            second(y // 2, y % 2, pair, 2 * (step % 2) + pair)
            if step >= 3:
                render(step - 3, pair)
        if step in (4, 6):
            pack(step // 2 - 2)
    for y in (5, 6, 7):
        for part in range(2):
            render(y, part)
        if y != 6:
            pack(y // 2)


def pair_kernel(keep, got, out):
    own_first = lax.axis_index("pencil") % 2 == lax.axis_index("slab") // 2
    first_half = lax.broadcasted_iota(jnp.int32, (32, 128), 1) < 64
    for slab in range(4):
        rows = [pl.ds(32 * (4 * channel + slab), 32) for channel in range(4)]
        own = [keep[at, :] for at in rows]
        other = [got[at, :] for at in rows]
        clear = jnp.exp(-jnp.where(own_first, own[3], other[3]))
        merged = []
        for channel in range(3):
            front = jnp.where(own_first, own[channel], other[channel])
            back = jnp.where(own_first, other[channel], own[channel])
            merged.append(front + clear * back)
        merged.append(own[3] + other[3])
        for row in range(2):
            low, high = merged[2 * row], merged[2 * row + 1]
            mixed = (
                jnp.where(first_half, low, pltpu.roll(high, 64, 1)),
                jnp.where(first_half, pltpu.roll(low, 64, 1), high),
            )
            for core in range(2):
                out[pl.ds(128 * slab + 2 * core + row, 32, stride=4), :] = mixed[core]


def blend_kernel(got, out):
    row = lax.broadcasted_iota(jnp.int32, (128, 128), 0)
    col = lax.broadcasted_iota(jnp.int32, (128, 128), 1)
    rank = jnp.where(row < 64, row, 191 - row)
    earlier = (jnp.where(col < 64, col, 191 - col) < rank).astype(BF16)
    for y in range(2):
        red_green = got[pl.ds(2 * y, 128, stride=4), :]
        blue_depth = got[pl.ds(2 * y + 1, 128, stride=4), :]
        depth = jnp.where(col < 64, pltpu.roll(blue_depth, 64, 1), blue_depth)
        high = depth.astype(BF16)
        rest = depth - high.astype(F32)
        middle = rest.astype(BF16)
        low = (rest - middle.astype(F32)).astype(BF16)
        before = straight(earlier, high) + straight(earlier, middle) + straight(earlier, low)
        clear = jnp.exp(-before)
        mixed = jnp.sum(clear * red_green, axis=0, keepdims=True)
        out[0, pl.ds(y, 1), :] = mixed[:, :64]
        out[1, pl.ds(y, 1), :] = mixed[:, 64:]
        out[2, pl.ds(y, 1), :] = jnp.sum(clear * blue_depth, axis=0, keepdims=True)[:, :64]
        opacity = 1.0 - jnp.exp(-jnp.sum(depth, axis=0, keepdims=True))
        out[3, pl.ds(y, 1), :] = opacity[:, :64]


def vmem_call(kernel, out_type, scratch=(), in_specs=None):
    params = pltpu.CompilerParams(vmem_limit_bytes=24 << 20)
    specs = {} if in_specs is None else {"in_specs": in_specs}
    return pl.pallas_call(
        kernel, out_shape=out_type, scratch_shapes=scratch, compiler_params=params, **specs
    )


def near(array):
    return pltpu.with_memory_space_constraint(array, pltpu.VMEM)


def pinned(array):
    return pltpu.with_memory_space_constraint(array, pltpu.HBM)


def x_call(spectrum):
    tables = [pinned(jnp.asarray(table)) for table in x_tables()]
    far = pl.BlockSpec(memory_space=pltpu.HBM)
    lines = pltpu.VMEM((2, 512, 512), BF16)
    matrix = pltpu.VMEM((512, 256), BF16)
    return vmem_call(
        x_kernel,
        pltpu.VMEM((4096, 128), F32),
        [
            pltpu.VMEM((2, 2, 32, 4096), F32),
            pltpu.VMEM((32, 256), F32),
            matrix,
            matrix,
            lines,
            lines,
            pltpu.SemaphoreType.DMA((7,)),
        ],
        [far] * 4,
    )(pinned(spectrum), *tables)


def z_call(got):
    tables = [jnp.asarray(table) for table in z_tables()]
    lines = pltpu.VMEM((4, 256, 256), BF16)
    return vmem_call(
        z_kernel,
        (pltpu.VMEM((512, 128), F32), pltpu.VMEM((512, 128), F32)),
        [pltpu.VMEM((16, 8, 32, 128), F32), lines, lines, pltpu.VMEM((4, 8, 32, 128), F32)],
    )(got, *tables)


def local(spectrum):
    blocks = x_call(spectrum).reshape(256, 16, 128)
    got = lax.all_to_all(blocks, AXES, split_axis=0, concat_axis=0, tiled=True)
    keep, give = z_call(near(got.reshape(4096, 128)))
    swap = [(i, i ^ 1) for i in range(lax.axis_size("pencil"))]
    other = near(lax.ppermute(give, "pencil", swap))
    blocks = vmem_call(pair_kernel, pltpu.VMEM((512, 128), F32))(near(keep), other)
    got = lax.all_to_all(
        blocks.reshape(256, 2, 128), AXES, split_axis=0, concat_axis=0, tiled=True
    )
    out_type = jax.ShapeDtypeStruct((4, 2, 64), F32)
    return vmem_call(blend_kernel, out_type)(near(got.reshape(512, 128)))


def solution(mesh):
    return jax.shard_map(
        local,
        mesh=mesh,
        in_specs=(P(None, "slab", "pencil", None),),
        out_specs=P(None, "slab", "pencil"),
        check_vma=False,
    )
```

```python
import math

import numpy as np

import jax
import jax.numpy as jnp
from jax import lax
from jax.experimental import pallas as pl
from jax.experimental.pallas import tpu as pltpu
from jax.sharding import PartitionSpec as P

N = 4096
LOG2E = math.log2(math.e)
AXES = ("slab", "pencil")
F32 = jnp.float32
BF16 = jnp.bfloat16


def split_np(table):
    high = table.astype(np.float32).astype(BF16)
    low = (table - high.astype(np.float64)).astype(np.float32).astype(BF16)
    return high, low


def split(value):
    high = value.astype(BF16)
    low = (value - high.astype(F32)).astype(BF16)
    return high, low


def complex_block(phase):
    cosine, sine = np.cos(phase), np.sin(phase)
    return np.block([[cosine, -sine], [sine, cosine]])


def x_tables():
    lines = np.arange(256)
    phase = 2 * np.pi * ((2 * np.arange(128) + 1)[:, None] * lines[None, :] % 512) / 512
    cosine, sine = np.cos(phase), np.sin(phase)
    matrix = np.stack([[cosine, sine], [-sine, cosine]]).transpose(0, 2, 1, 3).reshape(512, 256)
    fine = 2 * np.pi * ((np.arange(16) - 8)[:, None] * lines[None, :] % N) / N
    twist = np.stack([np.cos(fine), np.sin(fine)], axis=1).reshape(32, 256)
    return (twist.astype(np.float32),) + split_np(matrix)


def z_tables():
    outer = np.arange(128)[:, None] * np.arange(64)[None, :]
    first = complex_block(2 * np.pi * (outer % 128) / 128) / 4096
    fine = 2 * np.pi * (np.arange(128)[:, None] * (np.arange(128) % 32)[None, :] % N) / N
    twist = np.stack([np.cos(fine), np.sin(fine)])
    short = 2 * np.pi * (np.arange(32)[:, None] * np.arange(32)[None, :] % 32) / 32
    second = np.concatenate(
        [np.kron(np.eye(4), np.cos(short)), -np.kron(np.eye(4), np.sin(short))], axis=1
    )
    first = first.reshape(256, 2, 64).transpose(0, 2, 1).reshape(256, 128)
    first = np.stack([first, first * np.where(np.arange(128) % 2, -1.0, 1.0)])
    first_high, first_low = split_np(first)
    first_both = np.concatenate([first_high, first_high], axis=2)
    second_all = np.concatenate(split_np(second), axis=0)
    return (first_both, first_low, twist.astype(np.float32), second_all)


def four(a, b, c, d):
    (ar, ai), (br, bi), (cr, ci), (dr, di) = a, b, c, d
    er, ei, fr, fi = ar + cr, ai + ci, ar - cr, ai - ci
    gr, gi, hr, hi = br + dr, bi + di, br - dr, bi - di
    return [(er + gr, ei + gi), (fr - hi, fi + hr), (er - gr, ei - gi), (fr + hi, fi - hr)]


def turned(value, steps):
    re, im = value
    if steps == 0:
        return value
    if steps == 4:
        return (-im, re)
    half = math.sqrt(0.5)
    if steps == 2:
        return ((re - im) * half, (re + im) * half)
    if steps == 6:
        return ((-re - im) * half, (re - im) * half)
    c, s = math.cos(math.pi * steps / 8), math.sin(math.pi * steps / 8)
    return (re * c - im * s, re * s + im * c)


def x_kernel(
    data, twist_hbm, high_hbm, low_hbm, out, cells_v, twist, high_w, low_w, high_t, low_t, sems
):
    copies = [pltpu.make_async_copy(twist_hbm, twist, sems.at[0])]
    for y in range(2):
        for half in range(2):
            rows = pl.ds(16 * half, 16)
            copies.append(
                pltpu.make_async_copy(
                    data.at[:, y, rows, :], cells_v.at[:, y, rows, :], sems.at[1 + 2 * y + half]
                )
            )
    copies.append(pltpu.make_async_copy(high_hbm, high_w, sems.at[5]))
    copies.append(pltpu.make_async_copy(low_hbm, low_w, sems.at[6]))
    for index in (1, 0, 2, 5, 6, 3, 4):
        copies[index].start()

    def stage(y, half, tile):
        rows, lanes = pl.ds(16 * half, 16), pl.ds(128 * tile, 128)
        cells = [
            tuple(cells_v[part, y, rows, pl.ds(256 * t + 128 * tile, 128)] for part in range(2))
            for t in range(16)
        ]
        middle = [four(*(cells[4 * t1 + t0] for t1 in range(4))) for t0 in range(4)]
        for k1 in range(4):
            ends = four(*(turned(middle[t0][k1], t0 * k1) for t0 in range(4)))
            for k0 in range(4):
                fine = k1 + 4 * k0
                value = ends[k0]
                if fine != 8:
                    re, im = value
                    c = twist[pl.ds(2 * fine, 1), lanes]
                    s = twist[pl.ds(2 * fine + 1, 1), lanes]
                    value = (re * c - im * s, re * s + im * c)
                for part in range(2):
                    high, low = split(value[part])
                    at = pl.ds(32 * fine + 16 * half, 16)
                    columns = pl.ds(256 * part + 128 * tile, 128)
                    high_t[y, at, columns] = high
                    low_t[y, at, columns] = low

    def send(y, pair):
        rows = pl.ds(256 * pair, 256)
        parts = []
        for part in range(2):
            at = pl.ds(256 * part, 256)
            high, low = high_t[y, rows, at], low_t[y, rows, at]
            value = across(high_w[at], high) + across(low_w[at], high) + across(high_w[at], low)
            parts.append(value)
        for side, value in enumerate((parts[0] + parts[1], parts[0] - parts[1])):
            for k in range(2):
                at = pl.ds(2048 * side + 4 * y + 2 * pair + k, 256, stride=8)
                out[at, :] = value[:, 128 * k : 128 * k + 128]

    copies[0].wait()
    for half in range(2):
        copies[1 + half].wait()
        for tile in range(2):
            stage(0, half, tile)
    for index in (5, 6, 3):
        copies[index].wait()
    for pair in range(2):
        send(0, pair)
        stage(1, 0, pair)
    copies[4].wait()
    for tile in range(2):
        stage(1, 1, tile)
    for pair in range(2):
        send(1, pair)


def across(left, right):
    return lax.dot_general(left, right, (((1,), (1,)), ((), ())), preferred_element_type=F32)


def straight(left, right):
    return lax.dot_general(left, right, (((1,), (0,)), ((), ())), preferred_element_type=F32)


def z_kernel(
    got, first_both, first_low, twist, second_all, keep, give, field, high_q, low_q, image
):
    mirrored = lax.axis_index("slab") // 2
    core = lax.axis_index("pencil") % 2
    lane = lax.broadcasted_iota(jnp.int32, (8, 128), 1)
    mode = lax.broadcasted_iota(jnp.int32, (8, 128), 0) // 2
    weight = jnp.where((mode == 0) & (lane % 32 == 0), 0.5, 1.0).astype(F32)

    def first(slab, y, pair, slot):
        blocks = []
        for k in range(2):
            row = slab * 1024 + 4 * y + 2 * pair + k
            head = got[pl.ds(row, 8, stride=8), :] * weight
            blocks.append(jnp.concatenate([head, got[pl.ds(row + 64, 120, stride=8), :]], axis=0))
        high, low = split(jnp.concatenate(blocks, axis=1))
        value = straight(first_both[mirrored], jnp.concatenate([high, low], axis=0))
        value = value + straight(first_low[mirrored], high)
        for part in range(2):
            half = pl.ds(64 * part, 64)
            c, s = twist[0, half], twist[1, half]
            for k in range(2):
                lanes = slice(128 * k, 128 * k + 128)
                r = value[64 * part : 64 * part + 64, lanes]
                i = value[128 + 64 * part : 192 + 64 * part, lanes]
                at = pl.ds(128 * k + 64 * part, 64)
                for column, turned_value in enumerate((r * c - i * s, r * s + i * c)):
                    columns = pl.ds(128 * column, 128)
                    high, low = split(turned_value)
                    high_q[slot, at, columns] = high
                    low_q[slot, at, columns] = low

    def second(slab, y, pair, slot):
        both = across(second_all[...], high_q[slot])
        value = both[:128] + both[128:] + across(second_all[pl.ds(0, 128)], low_q[slot])
        for k in range(2):
            for near in range(4):
                field[4 * (2 * pair + k) + near, 2 * slab + y] = value[
                    32 * near : 32 * near + 32, 128 * k : 128 * k + 128
                ]

    first_half = lax.broadcasted_iota(jnp.int32, (32, 128), 1) < 64

    def render(y, part):
        rows = pl.ds(16 * part, 16)
        before, after = (y + 7) % 8, (y + 1) % 8
        zero = jnp.zeros((16, 128), F32)
        clear, depth, total, tilted, glow = jnp.ones((16, 128), F32), zero, zero, zero, zero
        for x in range(16):
            half = field[x, y, rows]
            shading = 2.0 + jnp.tanh(field[x, after, rows] - field[x, before, rows])
            square = half * half
            passed = clear * jnp.exp2(square * (-4.0 * LOG2E / N))
            weight = (clear - passed) * shading
            clear = passed
            depth = depth + square
            total = total + weight
            tilted = tilted + weight * jnp.tanh(3.0 * half)
            glow = glow + weight * jnp.exp2(square * (-4.0 * LOG2E))
        red = 0.25 * (total + tilted)
        image[0, y, rows] = red
        image[1, y, rows] = 0.25 * glow
        image[2, y, rows] = 0.5 * total - red
        image[3, y, rows] = depth * (4.0 / N)

    def pack(slab):
        for channel in range(4):
            low, high = image[channel, 2 * slab], image[channel, 2 * slab + 1]
            mixed = (
                jnp.where(first_half, low, pltpu.roll(high, 64, 1)),
                jnp.where(first_half, pltpu.roll(low, 64, 1), high),
            )
            at = pl.ds(32 * (4 * channel + slab), 32)
            keep[at, :] = jnp.where(core == 0, mixed[0], mixed[1])
            give[at, :] = jnp.where(core == 0, mixed[1], mixed[0])

    order = (7, 0, 1, 2, 3, 4, 5, 6)
    for pair in range(2):
        first(order[0] // 2, order[0] % 2, pair, pair)
    for step in range(8):
        for pair in range(2):
            if step < 7:
                y = order[step + 1]
                first(y // 2, y % 2, pair, 2 - 2 * (step % 2) + pair)
            y = order[step]
            second(y // 2, y % 2, pair, 2 * (step % 2) + pair)
            if step >= 3:
                render(step - 3, pair)
        if step in (4, 6):
            pack(step // 2 - 2)
    for y in (5, 6, 7):
        for part in range(2):
            render(y, part)
        if y != 6:
            pack(y // 2)


def pair_kernel(keep, got, out):
    own_first = lax.axis_index("pencil") % 2 == lax.axis_index("slab") // 2
    for slab in range(4):
        own = [keep[pl.ds(32 * (4 * channel + slab), 32), :] for channel in range(4)]
        other = [got[pl.ds(32 * (4 * channel + slab), 32), :] for channel in range(4)]
        clear = jnp.exp(-jnp.where(own_first, own[3], other[3]))
        for channel in range(4):
            if channel == 3:
                value = own[3] + other[3]
            else:
                front = jnp.where(own_first, own[channel], other[channel])
                back = jnp.where(own_first, other[channel], own[channel])
                value = front + clear * back
            out[pl.ds(128 * slab + channel, 32, stride=4), :] = value


def blend_kernel(got, out):
    depth = got[pl.ds(3, 128, stride=4), :]
    row = lax.broadcasted_iota(jnp.int32, (128, 128), 0)
    col = lax.broadcasted_iota(jnp.int32, (128, 128), 1)
    rank = jnp.where(row < 64, row, 191 - row)
    earlier = (jnp.where(col < 64, col, 191 - col) < rank).astype(BF16)
    high = depth.astype(BF16)
    rest = depth - high.astype(F32)
    middle = rest.astype(BF16)
    low = (rest - middle.astype(F32)).astype(BF16)
    before = straight(earlier, high) + straight(earlier, middle) + straight(earlier, low)
    clear = jnp.exp(-before)
    rows = [
        jnp.sum(clear * got[pl.ds(channel, 128, stride=4), :], axis=0, keepdims=True)
        for channel in range(3)
    ]
    rows.append(1.0 - jnp.exp(-jnp.sum(depth, axis=0, keepdims=True)))
    for channel in range(4):
        for y in range(2):
            out[channel, pl.ds(y, 1), :] = rows[channel][:, 64 * y : 64 * y + 64]


def vmem_call(kernel, out_type, scratch=(), in_specs=None):
    params = pltpu.CompilerParams(vmem_limit_bytes=24 << 20)
    specs = {} if in_specs is None else {"in_specs": in_specs}
    return pl.pallas_call(
        kernel, out_shape=out_type, scratch_shapes=scratch, compiler_params=params, **specs
    )


def near(array):
    return pltpu.with_memory_space_constraint(array, pltpu.VMEM)


def pinned(array):
    return pltpu.with_memory_space_constraint(array, pltpu.HBM)


def x_call(spectrum):
    tables = [pinned(jnp.asarray(table)) for table in x_tables()]
    far = pl.BlockSpec(memory_space=pltpu.HBM)
    lines = pltpu.VMEM((2, 512, 512), BF16)
    matrix = pltpu.VMEM((512, 256), BF16)
    return vmem_call(
        x_kernel,
        pltpu.VMEM((4096, 128), F32),
        [
            pltpu.VMEM((2, 2, 32, 4096), F32),
            pltpu.VMEM((32, 256), F32),
            matrix,
            matrix,
            lines,
            lines,
            pltpu.SemaphoreType.DMA((7,)),
        ],
        [far] * 4,
    )(pinned(spectrum), *tables)


def z_call(got):
    tables = [jnp.asarray(table) for table in z_tables()]
    lines = pltpu.VMEM((4, 256, 256), BF16)
    return vmem_call(
        z_kernel,
        (pltpu.VMEM((512, 128), F32), pltpu.VMEM((512, 128), F32)),
        [pltpu.VMEM((16, 8, 32, 128), F32), lines, lines, pltpu.VMEM((4, 8, 32, 128), F32)],
    )(got, *tables)


def local(spectrum):
    blocks = x_call(spectrum).reshape(256, 16, 128)
    got = lax.all_to_all(blocks, AXES, split_axis=0, concat_axis=0, tiled=True)
    keep, give = z_call(near(got.reshape(4096, 128)))
    swap = [(i, i ^ 1) for i in range(lax.axis_size("pencil"))]
    other = near(lax.ppermute(give, "pencil", swap))
    blocks = vmem_call(pair_kernel, pltpu.VMEM((512, 128), F32))(near(keep), other)
    same_core = [[2 * i + core for i in range(128)] for core in range(2)]
    got = lax.all_to_all(
        blocks.reshape(128, 4, 128),
        AXES,
        split_axis=0,
        concat_axis=0,
        axis_index_groups=same_core,
        tiled=True,
    )
    out_type = jax.ShapeDtypeStruct((4, 2, 64), F32)
    return vmem_call(blend_kernel, out_type)(near(got.reshape(512, 128)))


def solution(mesh):
    return jax.shard_map(
        local,
        mesh=mesh,
        in_specs=(P(None, "slab", "pencil", None),),
        out_specs=P(None, "slab", "pencil"),
        check_vma=False,
    )
```
